32 devices in a mesh: groups: 2 (over x), row: 16 (over z, y, core).
Axes of the slice: x: 2, y: 2, z: 4, core: 2. Of those that a mesh axis runs over, the one named last changes fastest.
Arguments:
- atom_feat: bfloat16 [8192, 128], P(('groups', 'row')), parts along dimension 0, may hold values from -8 to 8
- window_start: int32 [256], P(('groups', 'row')), parts along dimension 0, may hold values from -64 to 4032, as said below
- atom_count: int32 [512], P(('groups', 'row')), parts along dimension 0, may hold values from 1 to 24, as said below
- residue_type: int32 [512], P(('groups', 'row')), parts along dimension 0, may hold values from 0 to 31
- chain_id: int32 [512], P(('groups', 'row')), parts along dimension 0, may hold values from 0 to 5, never falling along the last dimension, each value on 1 to 64 neighbouring positions
- token_single: bfloat16 [512, 768], P(('groups', 'row')), parts along dimension 0, may hold values from -6 to 6
- pair: bfloat16 [512, 256, 128], P(('groups', 'row')), parts along dimension 0, may hold values from -8 to 8
- atom_gain: float32 [128], replicated, may hold values from 0.25 to 1.75
- atom_qkv: bfloat16 [128, 384], replicated, may hold values from -1 to 1
- atom_out: bfloat16 [128, 128], replicated, may hold values from -0.5 to 0.5
- pool_weight: bfloat16 [128, 768], replicated, may hold values from -0.5 to 0.5
- restype_table: bfloat16 [32, 768], replicated, may hold values from -3 to 3
- token_gain: float32 [768], replicated, may hold values from 0.25 to 1.75
- token_proj: bfloat16 [768, 3072], replicated, may hold values from -0.21875 to 0.21875
- token_out: bfloat16 [768, 768], replicated, may hold values from -0.21875 to 0.21875
- pair_gain: float32 [128], replicated, may hold values from 0.1 to 1.9
- pair_bias_weight: bfloat16 [128, 16], replicated, may hold values from -16 to 16
- chain_weight: float32 [16], replicated, may hold values from -2 to 2
- back_weight: bfloat16 [768, 128], replicated, may hold values from -0.21875 to 0.21875
Outputs:
- atoms_out: bfloat16 [8192, 128], P(('groups', 'row')), parts along dimension 0
- tokens_out: bfloat16 [512, 768], P(('groups', 'row')), parts along dimension 0
The draws below stay inside these ranges and needn't reach their ends.
There are 2 independent parts, one for each index of `groups`. The reference program is written for one: setup_inputs(seed, part) draws one part's arguments, and reference() takes and returns one part's arrays. A program takes and returns all parts, laid end to end along the dimension named above; an argument that names none is the same for every part. Nothing has to cross between parts.
Inputs may be any that keep to these rules, and one draw needn't show every extreme that they name: `window_start`: key window b begins within 16 of b * 32 + 32 // 2 - 128 // 2. `atom_count`: atoms of token t follow those of token t - 1 and the counts sum to 4096; for every k, the first atom of token k * 16 lies within 64 of atom k * 256. `chain_id`: chain numbers never fall along the tokens.
All inputs are finite; a program needn't handle non-finite values.
Results may differ from the reference program's by a relative error of at most 0.008.
Values may be sent and summed in bfloat16 or wider, within the bound.
A program may use at most 64 MiB of HBM per device.

```python
import math
import jax
import jax.numpy as jnp
import numpy as np
from jax import lax

CA = 128
CS = 768
CZ = 128
HEADS = 16
AHEADS = 4
RESTYPES = 32
QBLK = 32
KWIN = 128
JITTER = 16
MOSTA = 24
CHAINS = 6
ATOM_DEV = 256
TOK_DEV = 16
HDIM = 48
ADIM = 32
HALO = 64
DRIFT = 64
NA = 4096
NT = 256
NW = 128


def draw_window_start(key, part):
    blocks = jnp.arange(NA // QBLK, dtype=jnp.int32)
    jitters = jax.random.randint(key, (NA // QBLK,), -JITTER, JITTER + 1, dtype=jnp.int32)
    return blocks * QBLK + QBLK // 2 - KWIN // 2 + jitters


def draw_atom_count(key, part):
    key = jax.random.fold_in(key, 11)
    pick_key, drift_key, spot_key, weight_key, order_key = jax.random.split(key, 5)
    owners = NT // TOK_DEV
    top = MOSTA - 1
    chosen = jax.random.randint(pick_key, (), 1, owners - 1, dtype=jnp.int32)
    marks = jnp.arange(owners + 1, dtype=jnp.int32)
    offsets = jax.random.randint(drift_key, (owners + 1,), -DRIFT, DRIFT + 1, dtype=jnp.int32)
    offsets = jnp.where(marks == chosen, -DRIFT, offsets)
    offsets = jnp.where(marks == chosen + 1, DRIFT, offsets)
    offsets = jnp.where((marks == 0) | (marks == owners), 0, offsets)
    totals = ATOM_DEV + offsets[1:] - offsets[:-1]
    slots = jnp.arange(TOK_DEV, dtype=jnp.int32)
    spots = jax.random.randint(spot_key, (owners, 1), 0, TOK_DEV, dtype=jnp.int32)
    reserved = (marks[:owners, None] == chosen) & (slots[None, :] == spots)
    reserved_int = reserved.astype(jnp.int32)
    weights = jnp.where(reserved, 0, jax.random.randint(weight_key, (owners, TOK_DEV), 1, 5, dtype=jnp.int32))
    remain = totals - TOK_DEV - top * jnp.sum(reserved_int, axis=1)
    share = jnp.minimum(top, remain[:, None] * weights // jnp.sum(weights, axis=1, keepdims=True))
    room = jnp.where(reserved, 0, top - share)
    leftover = remain - jnp.sum(share, axis=1)
    ranking = jax.random.randint(order_key, (owners, TOK_DEV), 0, 1024, dtype=jnp.int32) * TOK_DEV + slots[None, :]
    order = jnp.argsort(ranking, axis=1)
    room_sorted = jnp.take_along_axis(room, order, axis=1)
    before = jnp.cumsum(room_sorted, axis=1) - room_sorted
    extra_sorted = jnp.clip(leftover[:, None] - before, 0, room_sorted)
    extra = jnp.take_along_axis(extra_sorted, jnp.argsort(order, axis=1), axis=1)
    counts = 1 + share + extra + top * reserved_int
    return counts.reshape(NT).astype(jnp.int32)


def draw_atom_feat(key, part):
    key = jax.random.fold_in(key, 12)
    first = jax.random.fold_in(key, 0)
    values = jnp.clip(jax.random.normal(first, (NA, CA), jnp.float32), -6.0, 6.0)
    return values.astype(jnp.bfloat16)


def draw_atom_qkv(key, part):
    key = jax.random.fold_in(key, 14)
    matrix = jnp.clip(jax.random.normal(key, (CA, 3 * CA), jnp.float32), -4.0, 4.0) / math.sqrt(CA)
    return matrix.astype(jnp.bfloat16)


def draw_pair(key, part):
    key = jax.random.fold_in(key, 13)
    first = jax.random.fold_in(key, 0)
    values = jnp.clip(jax.random.normal(first, (NT, NT, CZ), jnp.float32), -6.0, 6.0)
    return values.astype(jnp.bfloat16)


def draw_pair_bias_weight(key, part):
    key = jax.random.fold_in(key, 15)
    matrix = 2.0 * jnp.clip(jax.random.normal(key, (CZ, HEADS), jnp.float32), -4.0, 4.0) / math.sqrt(CZ)
    return matrix.astype(jnp.bfloat16)


def place_ends(drawn, key, least, largest):
    longest = drawn.shape.index(max(drawn.shape))
    spots = []
    for shift in (0, 1):
        where = [jax.random.randint(jax.random.fold_in(key, axis), (), 0, length) for axis, length in enumerate(drawn.shape)]
        where[longest] = (where[longest] + shift) % drawn.shape[longest]
        spots.append(tuple(where))
    return drawn.at[spots[0]].set(least).at[spots[1]].set(largest)


def shard_levels(stream_key, dims, pieces, smallest, high):
    loudness, own = 1.0, jax.random.fold_in(stream_key, 6)
    for dim, blocks in pieces:
        heights = jnp.exp(jax.random.uniform(jax.random.fold_in(own, dim), (blocks,), jnp.float32, smallest / len(pieces), high / len(pieces)))
        loudness = loudness * jnp.repeat(heights, dims[dim] // blocks).reshape([-1 if axis == dim else 1 for axis in range(len(dims))])
    return loudness


def profile(amount, total, most, lean):
    loads = [(1 << 20) // math.isqrt(standing ** lean) + 1 for standing in range(2, amount + 1)]
    spare, given = total - most - (amount - 1), [1] * (amount - 1)
    while spare > 0:
        candidates = [i for i in range(amount - 1) if given[i] < most]
        mass, remaining = sum([loads[i] for i in candidates]), spare
        for i in candidates:
            more = min(most - given[i], max(1, remaining * loads[i] // mass), spare)
            given[i] = given[i] + more
            spare = spare - more
    return np.array([most] + given)


def uneven(own_key, amount, total, limit, slope):
    if amount == 2:
        one = jax.random.randint(own_key, (), max(1, total - limit), min(limit, total - 1) + 1)
        return jnp.stack([one, total - one])
    sizes = jnp.asarray(profile(amount, total, limit, slope), jnp.int32)
    twos = (amount - 1) // 2
    giver, taker = sizes[1:1 + 2 * twos:2], sizes[2:2 + 2 * twos:2]
    margin = jnp.minimum(giver - 1, limit - taker)
    shifted = jax.random.randint(jax.random.fold_in(own_key, 1), (twos,), 0, 1 << 20) % (margin + 1)
    sizes = sizes.at[1:1 + 2 * twos:2].set(giver - shifted).at[2:2 + 2 * twos:2].set(taker + shifted)
    return sizes[jax.random.permutation(jax.random.fold_in(own_key, 2), amount)]


def centred(own_key, extent, deviation, limit, pieces=(), kind=jnp.bfloat16):
    array = deviation * jax.random.normal(own_key, extent, jnp.float32)
    if pieces:
        array = array * shard_levels(own_key, extent, pieces, -0.22, 0.18)
    return jnp.clip(array, -limit, limit).astype(kind)


def setup_inputs(seed: int = 0, part: int = 0) -> dict:
    key_of = jax.random.split(jax.random.key(seed), 20)
    part_keys = jax.random.split(jax.random.fold_in(key_of[19], part), 20)
    atom_feat = draw_atom_feat(jax.random.fold_in(jax.random.fold_in(key_of[19], part), 71), part)
    window_start = draw_window_start(jax.random.fold_in(jax.random.fold_in(key_of[19], part), 71), part)
    atom_count = draw_atom_count(jax.random.fold_in(jax.random.fold_in(key_of[19], part), 71), part)
    residue_type = place_ends(jax.random.randint(part_keys[3], (NT,), 0, RESTYPES), jax.random.fold_in(part_keys[3], 1), 0, RESTYPES - 1).astype(jnp.int32)
    chain_id = jnp.searchsorted(jnp.cumsum(uneven(part_keys[4], CHAINS, NT, NT // 4, 1)), jnp.arange(NT), side="right").astype(jnp.int32)
    token_single = centred(part_keys[5], (NT, CS), 1.0, 6.0, ((0, 16),))
    pair = draw_pair(jax.random.fold_in(jax.random.fold_in(key_of[19], part), 71), part)
    atom_gain = jnp.clip(1.0 + 0.15 * jax.random.normal(key_of[7], (CA,), jnp.float32), 0.25, 1.75)
    atom_qkv = draw_atom_qkv(jax.random.fold_in(key_of[19], 71), part)
    atom_out = centred(key_of[9], (CA, CA), CA ** -0.5, 0.5)
    pool_weight = centred(key_of[10], (CA, CS), CA ** -0.5, 0.5)
    restype_table = centred(key_of[11], (RESTYPES, CS), 0.5, 3.0)
    token_gain = jnp.clip(1.0 + 0.15 * jax.random.normal(key_of[12], (CS,), jnp.float32), 0.25, 1.75)
    token_proj = centred(key_of[13], (CS, 4 * CS), CS ** -0.5, 0.21875)
    token_out = centred(key_of[14], (CS, CS), CS ** -0.5, 0.21875)
    pair_gain = jnp.clip(1.0 + 0.18 * jax.random.normal(key_of[15], (CZ,), jnp.float32), 0.1, 1.9)
    pair_bias_weight = draw_pair_bias_weight(jax.random.fold_in(key_of[19], 71), part)
    chain_weight = jnp.clip(jax.random.uniform(key_of[17], (HEADS,), jnp.float32, -2.0, 2.0), -2.0, 2.0)
    back_weight = centred(key_of[18], (CS, CA), CS ** -0.5, 0.21875)
    return {"atom_feat": atom_feat, "window_start": window_start, "atom_count": atom_count, "residue_type": residue_type, "chain_id": chain_id, "token_single": token_single, "pair": pair, "atom_gain": atom_gain, "atom_qkv": atom_qkv, "atom_out": atom_out, "pool_weight": pool_weight, "restype_table": restype_table, "token_gain": token_gain, "token_proj": token_proj, "token_out": token_out, "pair_gain": pair_gain, "pair_bias_weight": pair_bias_weight, "chain_weight": chain_weight, "back_weight": back_weight}


def layer_norm(values, gain):
    centered = values - lax.optimization_barrier(jnp.mean(values, axis=-1, keepdims=True))
    variance = lax.optimization_barrier(jnp.mean(centered * centered, axis=-1, keepdims=True))
    return centered * lax.rsqrt(variance + 1e-05) * gain

def window_attend(queries, windows, inside):
    blocks = queries.shape[0]
    keys = windows[:, :, :CA].reshape(blocks, KWIN, AHEADS, ADIM).astype(jnp.float32)
    values = windows[:, :, CA:].reshape(blocks, KWIN, AHEADS, ADIM).astype(jnp.float32)
    scores = jnp.einsum('bqhd,bkhd->bhqk', queries.astype(jnp.float32), keys) / math.sqrt(ADIM)
    scores = jnp.where(inside[:, None, None, :], scores, -1000000000.0)
    weights = jnp.exp(scores - lax.optimization_barrier(jnp.max(scores, axis=-1, keepdims=True)))
    denom = lax.optimization_barrier(jnp.sum(weights, axis=-1, keepdims=True))
    mixed = jnp.einsum('bhqk,bkhd->bqhd', weights.astype(jnp.bfloat16).astype(jnp.float32), values)
    mixed = mixed / jnp.transpose(denom, (0, 2, 1, 3))
    return mixed.reshape(blocks * QBLK, CA).astype(jnp.bfloat16)

def reference(atom_feat, window_start, atom_count, residue_type, chain_id, token_single, pair, atom_gain, atom_qkv, atom_out, pool_weight, restype_table, token_gain, token_proj, token_out, pair_gain, pair_bias_weight, chain_weight, back_weight):
    ends = jnp.cumsum(atom_count).astype(jnp.int32)
    atom_token = jnp.searchsorted(ends, jnp.arange(NA, dtype=jnp.int32), side='right').astype(jnp.int32)
    normed = layer_norm(atom_feat.astype(jnp.float32), atom_gain).astype(jnp.bfloat16)
    atom_proj = jnp.dot(normed, atom_qkv, preferred_element_type=jnp.float32).astype(jnp.bfloat16)
    queries = atom_proj[:, :CA].reshape(NW, QBLK, AHEADS, ADIM)
    keyvals = jnp.pad(atom_proj[:, CA:], ((HALO, HALO), (0, 0)))
    anchors = (window_start + HALO).astype(jnp.int32)
    windows = jax.vmap(lambda anchor: lax.dynamic_slice_in_dim(keyvals, anchor, KWIN, 0))(anchors)
    position = window_start[:, None] + jnp.arange(KWIN, dtype=jnp.int32)[None, :]
    inside = (position >= 0) & (position < NA)
    attended = window_attend(queries, windows, inside)
    atoms_mid = (atom_feat.astype(jnp.float32) + jnp.dot(attended, atom_out, preferred_element_type=jnp.float32)).astype(jnp.bfloat16)
    lifted = jax.nn.relu(jnp.dot(atoms_mid, pool_weight, preferred_element_type=jnp.float32)).astype(jnp.bfloat16)
    pooled = jax.ops.segment_sum(lifted.astype(jnp.float32), atom_token, num_segments=NT)
    onehot = (residue_type[:, None] == jnp.arange(RESTYPES, dtype=jnp.int32)[None, :]).astype(jnp.bfloat16)
    state = token_single.astype(jnp.float32) + pooled / atom_count[:, None].astype(jnp.float32)
    state = state + jnp.dot(onehot, restype_table, preferred_element_type=jnp.float32)
    token_normed = layer_norm(state, token_gain).astype(jnp.bfloat16)
    token_all = jnp.dot(token_normed, token_proj, preferred_element_type=jnp.float32)
    qkv_part = token_all[:, :3 * CS].astype(jnp.bfloat16).astype(jnp.float32)
    query = qkv_part[:, :CS].reshape(NT, HEADS, HDIM)
    keys = qkv_part[:, CS:2 * CS].reshape(NT, HEADS, HDIM)
    values = qkv_part[:, 2 * CS:].reshape(NT, HEADS, HDIM)
    gate = jax.nn.sigmoid(token_all[:, 3 * CS:])

    def pair_bias(rows):
        pair_normed = layer_norm(rows.astype(jnp.float32), pair_gain).astype(jnp.bfloat16)
        return jnp.einsum('tkc,ch->thk', pair_normed.astype(jnp.float32), pair_bias_weight.astype(jnp.float32))
    bias = lax.map(pair_bias, pair.reshape(NT // TOK_DEV, TOK_DEV, NT, CZ)).reshape(NT, HEADS, NT)
    same = (chain_id[:, None] == chain_id[None, :]).astype(jnp.float32)
    scores = jnp.einsum('thd,khd->thk', query, keys) / math.sqrt(HDIM) + bias
    scores = scores + chain_weight[None, :, None] * same[:, None, :]
    weights = jnp.exp(scores - lax.optimization_barrier(jnp.max(scores, axis=-1, keepdims=True)))
    denom = lax.optimization_barrier(jnp.sum(weights, axis=-1))
    mixed = jnp.einsum('thk,khd->thd', weights.astype(jnp.bfloat16).astype(jnp.float32), values) / denom[:, :, None]
    gated = (mixed.reshape(NT, CS) * gate).astype(jnp.bfloat16)
    tokens_out = (state + jnp.dot(gated, token_out, preferred_element_type=jnp.float32)).astype(jnp.bfloat16)
    back = jnp.dot(tokens_out, back_weight, preferred_element_type=jnp.float32).astype(jnp.bfloat16)
    atoms_out = (atoms_mid.astype(jnp.float32) + back[atom_token].astype(jnp.float32)).astype(jnp.bfloat16)
    return (atoms_out, tokens_out)
```

```python
import functools
import math

import jax
import jax.numpy as jnp
from jax import lax
from jax.experimental import pallas as pl
from jax.experimental.pallas import tpu as pltpu
from jax.sharding import PartitionSpec as P

CA = 128
CS = 768
HEADS = 16
AHEADS = 4
QBLK = 32
KWIN = 128
HDIM = 48
ADIM = 32
HALO = 64
SLAB = QBLK + 2 * HALO
LANES = 128
F32 = jnp.float32
BF16 = jnp.bfloat16


def iota(shape, dim):
    return lax.broadcasted_iota(jnp.int32, shape, dim)


def layer_norm(values, gain):
    centered = values - jnp.mean(values, axis=-1, keepdims=True)
    variance = jnp.mean(centered * centered, axis=-1, keepdims=True)
    return centered * lax.rsqrt(variance + 1e-05) * gain


def dot(a, b):
    return jnp.dot(a, b, preferred_element_type=F32)


def dot_t(a, b):
    return lax.dot_general(a, b, (((1,), (1,)), ((), ())), preferred_element_type=F32)


def kernel(
    n,
    meta_ref,
    feat_hbm,
    single_ref,
    pair_hbm,
    atom_gain_ref,
    atom_qkv_ref,
    atom_out_ref,
    pool_hbm,
    table_ref,
    token_gain_ref,
    proj_hbm,
    out_hbm,
    pair_gain_ref,
    pair_weight_ref,
    chain_weight_ref,
    back_hbm,
    atoms_out_ref,
    tokens_out_ref,
    meta_all,
    xbuf,
    pair_v,
    pool_v,
    proj_v,
    out_v,
    backw_v,
    bias_v,
    tok_all,
    back_v,
    local_sem,
    meta_send,
    meta_recv,
    halo_send,
    halo_recv,
    tok_send,
    tok_recv,
    back_send,
    back_recv,
):
    me = lax.axis_index("row")
    nxt = lax.rem(me + 1, n)
    prv = lax.rem(me + n - 1, n)
    rows = feat_hbm.shape[0]
    toks = single_ref.shape[0]
    blocks = rows // QBLK
    edge = 2 * HALO
    total_tokens = n * toks
    total_atoms = n * rows

    barrier = pltpu.get_barrier_semaphore()

    def greet(k, c):
        pl.semaphore_signal(barrier, inc=1, device_id={"row": lax.rem(me + k, n)})
        return c

    lax.fori_loop(1, n, greet, 0)

    locals_ = []
    for i, (src, dst) in enumerate(
        [
            (pair_hbm, pair_v),
            (feat_hbm, xbuf.at[pl.ds(edge, rows)]),
            (pool_hbm, pool_v),
            (proj_hbm, proj_v),
            (out_hbm, out_v),
            (back_hbm, backw_v),
        ]
    ):
        copy = pltpu.make_async_copy(src, dst, local_sem.at[i])
        copy.start()
        locals_.append(copy)
    meta_all[me] = meta_ref[...]
    back_v[...] = jnp.zeros_like(back_v)

    pl.semaphore_wait(barrier, n - 1)

    up = pltpu.make_async_remote_copy(
        src_ref=feat_hbm.at[pl.ds(rows - edge, edge)],
        dst_ref=xbuf.at[pl.ds(0, edge)],
        send_sem=halo_send.at[0],
        recv_sem=halo_recv.at[0],
        device_id={"row": nxt},
    )
    down = pltpu.make_async_remote_copy(
        src_ref=feat_hbm.at[pl.ds(0, edge)],
        dst_ref=xbuf.at[pl.ds(edge + rows, edge)],
        send_sem=halo_send.at[1],
        recv_sem=halo_recv.at[1],
        device_id={"row": prv},
    )
    up.start()
    down.start()

    def meta_copy(k, slot):
        return pltpu.make_async_remote_copy(
            src_ref=meta_ref,
            dst_ref=meta_all.at[slot],
            send_sem=meta_send.at[k],
            recv_sem=meta_recv.at[slot],
            device_id={"row": lax.rem(me + k, n)},
        )

    def tok_copy(k, slot):
        return pltpu.make_async_remote_copy(
            src_ref=tok_all.at[slot],
            dst_ref=tok_all.at[slot],
            send_sem=tok_send.at[k],
            recv_sem=tok_recv.at[slot],
            device_id={"row": lax.rem(me + k, n)},
        )

    def start_meta(k, c):
        meta_copy(k, me).start()
        return c

    lax.fori_loop(1, n, start_meta, 0)

    locals_[0].wait()
    pair_gain = pair_gain_ref[...]
    pair_weight = pair_weight_ref[...]

    def pair_step(t, c):
        normed = layer_norm(pair_v[t].astype(F32), pair_gain).astype(BF16)
        bias_v[t] = dot_t(pair_weight, normed)
        return c

    lax.fori_loop(0, toks, pair_step, 0)

    locals_[1].wait()
    up.wait_recv()
    down.wait_recv()

    def wait_meta(k, c):
        meta_copy(k, lax.rem(me + k, n)).wait_recv()
        return c

    lax.fori_loop(1, n, wait_meta, 0)

    ext = xbuf[...].astype(F32)
    normed = layer_norm(ext, atom_gain_ref[...]).astype(BF16)
    aproj = dot(normed, atom_qkv_ref[...]).astype(BF16)
    metas = {-1: meta_all[prv][0:1, :], 0: meta_all[me][0:1, :], 1: meta_all[nxt][0:1, :]}
    head_lane = iota((1, CA), 1) // ADIM
    key_lane = iota((1, SLAB), 1)
    mixed_blocks = []
    side = HALO // QBLK
    for i in range(-side, blocks + side):
        at = edge + i * QBLK
        which, inner = (-1, i + blocks) if i < 0 else ((1, i - blocks) if i >= blocks else (0, i))
        lane = 3 * toks + inner
        start = metas[which][:, lane : lane + 1]
        position = me * rows + (i * QBLK - HALO) + key_lane
        inside = (
            (position >= start)
            & (position < start + KWIN)
            & (position >= 0)
            & (position < total_atoms)
        )
        queries = aproj[at : at + QBLK, :CA]
        expanded = jnp.concatenate(
            [jnp.where(head_lane == h, queries, jnp.zeros_like(queries)) for h in range(AHEADS)],
            axis=0,
        )
        keys = aproj[at - HALO : at + QBLK + HALO, CA : 2 * CA]
        values = aproj[at - HALO : at + QBLK + HALO, 2 * CA :]
        scores = dot_t(expanded, keys) * (1.0 / math.sqrt(ADIM))
        scores = jnp.where(inside, scores, -1000000000.0)
        weights = jnp.exp(scores - jnp.max(scores, axis=-1, keepdims=True))
        denom = jnp.sum(weights, axis=-1, keepdims=True)
        full = dot(weights.astype(BF16), values) / denom
        mixed = jnp.zeros((QBLK, CA), F32)
        for h in range(AHEADS):
            mixed = jnp.where(head_lane == h, full[h * QBLK : (h + 1) * QBLK], mixed)
        mixed_blocks.append(mixed.astype(BF16))
    attended = jnp.concatenate(mixed_blocks, axis=0)
    mid = (ext[HALO : HALO + rows + 2 * HALO] + dot(attended, atom_out_ref[...])).astype(BF16)

    locals_[2].wait()
    lifted = jax.nn.relu(dot(mid, pool_v[...])).astype(BF16)

    meta_f = meta_all[:, 0, :].astype(F32)
    source = iota((n, LANES), 0)
    count_lane = iota((n, LANES), 1) < toks
    tok_row = iota((toks, LANES), 0)
    tok_lane = iota((toks, LANES), 1)

    def column(row, first):
        return jnp.sum(jnp.where(tok_lane == tok_row + first, row, 0.0), axis=1, keepdims=True)

    def spans(device, row):
        prior = jnp.where((source < device) & count_lane, meta_f, 0.0)
        prior = jnp.sum(jnp.sum(prior, axis=1, keepdims=True), axis=0, keepdims=True)
        begin = prior + jnp.sum(jnp.where(tok_lane < tok_row, row, 0.0), axis=1, keepdims=True)
        return begin, begin + column(row, 0)

    own_row = metas[0].astype(F32)
    begin, end = spans(me, own_row)
    place = (me * rows - HALO + iota((1, rows + 2 * HALO), 1)).astype(F32)
    select = ((place >= begin) & (place < end)).astype(F32).astype(BF16)
    pooled = dot(select, lifted)
    kinds = table_ref.shape[0]
    onehot = (
        (iota((toks, kinds), 1).astype(F32) == column(own_row, 2 * toks)).astype(F32).astype(BF16)
    )
    state = single_ref[...].astype(F32) + pooled / column(own_row, 0)
    state = state + dot(onehot, table_ref[...])
    token_normed = layer_norm(state, token_gain_ref[...]).astype(BF16)
    tok_all[me] = token_normed

    def start_tok(k, c):
        tok_copy(k, me).start()
        return c

    lax.fori_loop(1, n, start_tok, 0)

    locals_[3].wait()
    query = dot(token_normed, proj_v[:, :CS]).astype(BF16).astype(F32)
    gate = jax.nn.sigmoid(dot(token_normed, proj_v[:, 3 * CS :]))
    column_of = iota((HEADS, CS), 1)
    head_row = iota((HEADS, CS), 0) * HDIM
    head_mask = ((column_of >= head_row) & (column_of < head_row + HDIM)).astype(F32)
    expanded = (query[:, None, :] * head_mask[None, :, :]).reshape(toks * HEADS, CS).astype(BF16)

    shift = toks.bit_length() - 1
    token_of = iota((LANES, total_tokens), 1)
    pick = (iota((LANES, total_tokens), 0) == toks + (token_of & (toks - 1))).astype(F32)
    chains = dot(meta_f.astype(BF16), pick.astype(BF16))
    owner = iota((n, total_tokens), 1) >> shift
    chains = jnp.sum(
        jnp.where(owner == iota((n, total_tokens), 0), chains, 0.0), axis=0, keepdims=True
    )
    same = (chains == column(own_row, toks)).astype(F32)
    eye = iota((HEADS, HEADS), 0) == iota((HEADS, HEADS), 1)
    chain_weight = jnp.sum(
        jnp.where(eye, chain_weight_ref[...], 0.0), axis=1, keepdims=True
    )
    extra = bias_v[...] + same[:, None, :] * chain_weight[None, :, :]

    def wait_tok(k, c):
        tok_copy(k, lax.rem(me + k, n)).wait_recv()
        return c

    lax.fori_loop(1, n, wait_tok, 0)
    everyone = tok_all[...].reshape(total_tokens, CS)
    keys = dot(everyone, proj_v[:, CS : 2 * CS]).astype(BF16)
    scores = dot_t(expanded, keys) * (1.0 / math.sqrt(HDIM))
    scores = scores + extra.reshape(toks * HEADS, total_tokens)
    weights = jnp.exp(scores - jnp.max(scores, axis=-1, keepdims=True))
    denom = jnp.sum(weights, axis=-1, keepdims=True)
    values = dot(everyone, proj_v[:, 2 * CS : 3 * CS]).astype(BF16)
    product = dot(weights.astype(BF16), values) / denom
    mixed = jnp.sum(product.reshape(toks, HEADS, CS) * head_mask[None, :, :], axis=1)
    gated = (mixed * gate).astype(BF16)
    locals_[4].wait()
    tokens_out = (state + dot(gated, out_v[...])).astype(BF16)
    tokens_out_ref[...] = tokens_out
    locals_[5].wait()
    back = dot(tokens_out, backw_v[...]).astype(BF16)
    back_v[1] = back

    def back_copy(slot, sem, peer):
        return pltpu.make_async_remote_copy(
            src_ref=back_v.at[1],
            dst_ref=back_v.at[slot],
            send_sem=back_send.at[sem],
            recv_sem=back_recv.at[sem],
            device_id={"row": peer},
        )

    ahead = back_copy(0, 0, nxt)
    behind = back_copy(2, 1, prv)

    @pl.when(me < n - 1)
    def _():
        ahead.start()

    @pl.when(me > 0)
    def _():
        behind.start()

    place = (me * rows + iota((1, rows), 1)).astype(F32)
    selects = []
    for offset in (-1, 0, 1):
        begin, end = spans(me + offset, metas[offset].astype(F32))
        selects.append(((place >= begin) & (place < end)).astype(F32))
    select = jnp.concatenate(selects, axis=0).T.astype(BF16)

    @pl.when(me > 0)
    def _():
        ahead.wait_recv()

    @pl.when(me < n - 1)
    def _():
        behind.wait_recv()

    beside = back_v[...].reshape(3 * toks, CA)
    own_mid = mid[HALO : HALO + rows].astype(F32)
    atoms_out_ref[...] = (own_mid + dot(select, beside)).astype(BF16)

    up.wait_send()
    down.wait_send()

    def drain(k, c):
        meta_copy(k, me).wait_send()
        tok_copy(k, me).wait_send()
        return c

    lax.fori_loop(1, n, drain, 0)

    @pl.when(me < n - 1)
    def _():
        ahead.wait_send()

    @pl.when(me > 0)
    def _():
        behind.wait_send()


def shards(
    n,
    atom_feat,
    window_start,
    atom_count,
    residue_type,
    chain_id,
    token_single,
    pair,
    atom_gain,
    atom_qkv,
    atom_out,
    pool_weight,
    restype_table,
    token_gain,
    token_proj,
    token_out,
    pair_gain,
    pair_bias_weight,
    chain_weight,
    back_weight,
):
    rows, toks = atom_feat.shape[0], token_single.shape[0]
    packed = jnp.concatenate([atom_count, chain_id, residue_type, window_start])
    packed = jnp.pad(packed, (0, LANES - packed.shape[0]))
    meta = jnp.broadcast_to(packed[None, :], (8, LANES))
    vmem = pl.BlockSpec(memory_space=pltpu.VMEM)
    hbm = pl.BlockSpec(memory_space=pl.ANY)
    dma = pltpu.SemaphoreType.DMA
    return pl.pallas_call(
        functools.partial(kernel, n),
        out_shape=(
            jax.ShapeDtypeStruct((rows, CA), BF16),
            jax.ShapeDtypeStruct((toks, CS), BF16),
        ),
        in_specs=[
            vmem, hbm, vmem, hbm, vmem, vmem, vmem, hbm,
            vmem, vmem, hbm, hbm, vmem, vmem, vmem, hbm,
        ],
        out_specs=(vmem, vmem),
        scratch_shapes=[
            pltpu.VMEM((n, 8, LANES), jnp.int32),
            pltpu.VMEM((rows + 4 * HALO, CA), BF16),
            pltpu.VMEM(pair.shape, BF16),
            pltpu.VMEM(pool_weight.shape, BF16),
            pltpu.VMEM(token_proj.shape, BF16),
            pltpu.VMEM(token_out.shape, BF16),
            pltpu.VMEM(back_weight.shape, BF16),
            pltpu.VMEM((toks, HEADS, n * toks), F32),
            pltpu.VMEM((n, toks, CS), BF16),
            pltpu.VMEM((3, toks, CA), BF16),
            dma((6,)),
            dma((n,)),
            dma((n,)),
            dma((2,)),
            dma((2,)),
            dma((n,)),
            dma((n,)),
            dma((2,)),
            dma((2,)),
        ],
        compiler_params=pltpu.CompilerParams(collective_id=0, has_side_effects=True),
    )(
        meta,
        atom_feat,
        token_single,
        pair,
        atom_gain.reshape(1, -1),
        atom_qkv,
        atom_out,
        pool_weight,
        restype_table,
        token_gain.reshape(1, -1),
        token_proj,
        token_out,
        pair_gain.reshape(1, -1),
        pair_bias_weight.T,
        chain_weight.reshape(1, -1),
        back_weight,
    )


def solution(mesh):
    split = P(("groups", "row"))
    return jax.shard_map(
        functools.partial(shards, mesh.shape["row"]),
        mesh=mesh,
        in_specs=(split,) * 7 + (P(),) * 12,
        out_specs=(split, split),
        check_vma=False,
    )
```

```python
import functools
import math

import jax
import jax.numpy as jnp
from jax import lax
from jax.experimental import pallas as pl
from jax.experimental.pallas import tpu as pltpu
from jax.sharding import PartitionSpec as P

CA = 128
CS = 768
HEADS = 16
AHEADS = 4
QBLK = 32
KWIN = 128
HDIM = 48
ADIM = 32
HALO = 64
SLAB = QBLK + 2 * HALO
LANES = 128
F32 = jnp.float32
BF16 = jnp.bfloat16


def iota(shape, dim):
    return lax.broadcasted_iota(jnp.int32, shape, dim)


def layer_norm(values, gain):
    centered = values - jnp.mean(values, axis=-1, keepdims=True)
    variance = jnp.mean(centered * centered, axis=-1, keepdims=True)
    return centered * lax.rsqrt(variance + 1e-05) * gain


def dot(a, b):
    return jnp.dot(a, b, preferred_element_type=F32)


def dot_t(a, b):
    return lax.dot_general(a, b, (((1,), (1,)), ((), ())), preferred_element_type=F32)


NAMES = (
        "feat",
        "window",
        "count",
        "residue",
        "chain",
        "single",
        "pair",
        "atom_gain",
        "atom_qkv",
        "atom_out",
        "pool",
        "table",
        "token_gain",
        "proj",
        "out",
        "pair_gain",
        "pair_weight",
        "chain_weight",
        "back",
    )


def kernel(n, *refs):
    count = len(NAMES)
    hbm = dict(zip(NAMES, refs[:count]))
    atoms_out_ref, tokens_out_ref = refs[count : count + 2]
    v = dict(zip(NAMES, refs[count + 2 : 2 * count + 2]))
    (
        stage,
        meta_all,
        bias_v,
        tok_all,
        back_v,
        local_sem,
        meta_send,
        meta_recv,
        halo_send,
        halo_recv,
        tok_send,
        tok_recv,
        back_send,
        back_recv,
    ) = refs[2 * count + 2 :]
    xbuf = v["feat"]
    feat_hbm = hbm["feat"]
    me = lax.axis_index("row")
    nxt = lax.rem(me + 1, n)
    prv = lax.rem(me + n - 1, n)
    rows = feat_hbm.shape[0]
    toks = hbm["single"].shape[0]
    blocks = rows // QBLK
    edge = 2 * HALO
    total_tokens = n * toks
    total_atoms = n * rows

    barrier = pltpu.get_barrier_semaphore()

    def greet(k, c):
        pl.semaphore_signal(barrier, inc=1, device_id={"row": lax.rem(me + k, n)})
        return c

    lax.fori_loop(1, n, greet, 0)

    loads = {}
    order = (
        "pair",
        "pair_gain",
        "pair_weight",
        "count",
        "chain",
        "window",
        "residue",
        "feat",
        "atom_gain",
        "atom_qkv",
        "atom_out",
        "pool",
        "single",
        "table",
        "token_gain",
        "chain_weight",
        "proj",
        "out",
        "back",
    )
    for i, name in enumerate(order):
        dst = xbuf.at[pl.ds(edge, rows)] if name == "feat" else v[name]
        loads[name] = pltpu.make_async_copy(hbm[name], dst, local_sem.at[i])
        loads[name].start()
    back_v[...] = jnp.zeros_like(back_v)
    stage[...] = jnp.zeros_like(stage)
    for i, name in enumerate(("count", "chain", "window", "residue")):
        loads[name].wait()
        value = v[name][...]
        stage[i : i + 1, : value.shape[1]] = value
    meta_all[me] = stage[...]

    loads["pair"].wait()
    loads["pair_gain"].wait()
    loads["pair_weight"].wait()
    pair_gain = v["pair_gain"][...]
    pair_weight = v["pair_weight"][...]

    def pair_step(t, c):
        normed = layer_norm(v["pair"][t].astype(F32), pair_gain).astype(BF16)
        bias_v[t] = dot_t(pair_weight, normed)
        return c

    first, second = toks // 4, toks // 2
    lax.fori_loop(0, first, pair_step, 0, unroll=4)
    pl.semaphore_wait(barrier, n - 1)

    up = pltpu.make_async_remote_copy(
        src_ref=feat_hbm.at[pl.ds(rows - edge, edge)],
        dst_ref=xbuf.at[pl.ds(0, edge)],
        send_sem=halo_send.at[0],
        recv_sem=halo_recv.at[0],
        device_id={"row": nxt},
    )
    down = pltpu.make_async_remote_copy(
        src_ref=feat_hbm.at[pl.ds(0, edge)],
        dst_ref=xbuf.at[pl.ds(edge + rows, edge)],
        send_sem=halo_send.at[1],
        recv_sem=halo_recv.at[1],
        device_id={"row": prv},
    )
    up.start()
    down.start()

    def meta_copy(k, slot):
        return pltpu.make_async_remote_copy(
            src_ref=stage,
            dst_ref=meta_all.at[slot],
            send_sem=meta_send.at[k],
            recv_sem=meta_recv.at[slot],
            device_id={"row": lax.rem(me + k, n)},
        )

    def tok_copy(k, slot):
        return pltpu.make_async_remote_copy(
            src_ref=tok_all.at[slot],
            dst_ref=tok_all.at[slot],
            send_sem=tok_send.at[k],
            recv_sem=tok_recv.at[slot],
            device_id={"row": lax.rem(me + k, n)},
        )

    def start_meta(k, c):
        meta_copy(k, me).start()
        return c

    lax.fori_loop(1, n, start_meta, 0)

    lax.fori_loop(first, second, pair_step, 0, unroll=4)

    for name in ("feat", "atom_gain", "atom_qkv", "atom_out", "pool"):
        loads[name].wait()
    up.wait_recv()
    down.wait_recv()

    def wait_meta(k, c):
        meta_copy(k, lax.rem(me + k, n)).wait_recv()
        return c

    lax.fori_loop(1, n, wait_meta, 0)

    ext = xbuf[...].astype(F32)
    normed = layer_norm(ext, v["atom_gain"][...]).astype(BF16)
    aproj = dot(normed, v["atom_qkv"][...]).astype(BF16)
    metas = {-1: meta_all[prv], 0: meta_all[me], 1: meta_all[nxt]}
    head_lane = iota((1, CA), 1) // ADIM
    key_lane = iota((1, SLAB), 1)
    mixed_blocks = []
    side = HALO // QBLK
    for i in range(-side, blocks + side):
        at = edge + i * QBLK
        which, inner = (-1, i + blocks) if i < 0 else ((1, i - blocks) if i >= blocks else (0, i))
        start = metas[which][2:3, inner : inner + 1]
        position = me * rows + (i * QBLK - HALO) + key_lane
        inside = (
            (position >= start)
            & (position < start + KWIN)
            & (position >= 0)
            & (position < total_atoms)
        )
        queries = aproj[at : at + QBLK, :CA]
        expanded = jnp.concatenate(
            [jnp.where(head_lane == h, queries, jnp.zeros_like(queries)) for h in range(AHEADS)],
            axis=0,
        )
        keys = aproj[at - HALO : at + QBLK + HALO, CA : 2 * CA]
        values = aproj[at - HALO : at + QBLK + HALO, 2 * CA :]
        scores = dot_t(expanded, keys) * (1.0 / math.sqrt(ADIM))
        scores = jnp.where(inside, scores, -1000000000.0)
        weights = jnp.exp(scores - jnp.max(scores, axis=-1, keepdims=True))
        denom = jnp.sum(weights, axis=-1, keepdims=True)
        full = dot(weights.astype(BF16), values) / denom
        mixed = jnp.zeros((QBLK, CA), F32)
        for h in range(AHEADS):
            mixed = jnp.where(head_lane == h, full[h * QBLK : (h + 1) * QBLK], mixed)
        mixed_blocks.append(mixed.astype(BF16))
    attended = jnp.concatenate(mixed_blocks, axis=0)
    mid = (ext[HALO : HALO + rows + 2 * HALO] + dot(attended, v["atom_out"][...])).astype(BF16)

    lifted = jax.nn.relu(dot(mid, v["pool"][...])).astype(BF16)

    counts_f = meta_all[:, 0, :].astype(F32)
    source = iota((n, LANES), 0)
    count_lane = iota((n, LANES), 1) < toks
    tok_row = iota((toks, LANES), 0)
    tok_lane = iota((toks, LANES), 1)

    def column(row):
        return jnp.sum(jnp.where(tok_lane == tok_row, row, 0.0), axis=1, keepdims=True)

    def spans(device, row):
        prior = jnp.where((source < device) & count_lane, counts_f, 0.0)
        prior = jnp.sum(jnp.sum(prior, axis=1, keepdims=True), axis=0, keepdims=True)
        begin = prior + jnp.sum(jnp.where(tok_lane < tok_row, row, 0.0), axis=1, keepdims=True)
        return begin, begin + column(row)

    own_meta = metas[0].astype(F32)
    own_row = own_meta[0:1]
    begin, end = spans(me, own_row)
    place = (me * rows - HALO + iota((1, rows + 2 * HALO), 1)).astype(F32)
    select = ((place >= begin) & (place < end)).astype(F32).astype(BF16)
    pooled = dot(select, lifted)
    kinds = hbm["table"].shape[0]
    onehot = (
        (iota((toks, kinds), 1).astype(F32) == column(own_meta[3:4])).astype(F32).astype(BF16)
    )
    for name in ("single", "table", "token_gain", "chain_weight"):
        loads[name].wait()
    state = v["single"][...].astype(F32) + pooled / column(own_row)
    state = state + dot(onehot, v["table"][...])
    gain = v["token_gain"][...]
    gain = jnp.concatenate([gain[i : i + 1] for i in range(gain.shape[0])], axis=1)
    token_normed = layer_norm(state, gain).astype(BF16)
    tok_all[me] = token_normed

    def start_tok(k, c):
        tok_copy(k, me).start()
        return c

    lax.fori_loop(1, n, start_tok, 0)

    loads["proj"].wait()
    proj_v = v["proj"]
    query = dot(token_normed, proj_v[:, :CS]).astype(BF16).astype(F32)
    gate = jax.nn.sigmoid(dot(token_normed, proj_v[:, 3 * CS :]))
    column_of = iota((HEADS, CS), 1)
    head_row = iota((HEADS, CS), 0) * HDIM
    head_mask = ((column_of >= head_row) & (column_of < head_row + HDIM)).astype(F32)
    expanded = (query[:, None, :] * head_mask[None, :, :]).reshape(toks * HEADS, CS).astype(BF16)

    shift = toks.bit_length() - 1
    token_of = iota((LANES, total_tokens), 1)
    pick = (iota((LANES, total_tokens), 0) == (token_of & (toks - 1))).astype(F32)
    chains = dot(meta_all[:, 1, :].astype(F32).astype(BF16), pick.astype(BF16))
    owner = iota((n, total_tokens), 1) >> shift
    chains = jnp.sum(
        jnp.where(owner == iota((n, total_tokens), 0), chains, 0.0), axis=0, keepdims=True
    )
    same = (chains == column(own_meta[1:2])).astype(F32)
    eye = iota((HEADS, HEADS), 0) == iota((HEADS, HEADS), 1)
    chain_weight = jnp.sum(
        jnp.where(eye, v["chain_weight"][...], 0.0), axis=1, keepdims=True
    )
    lax.fori_loop(second, toks, pair_step, 0, unroll=4)
    extra = bias_v[...] + same[:, None, :] * chain_weight[None, :, :]

    def wait_tok(k, c):
        tok_copy(k, lax.rem(me + k, n)).wait_recv()
        return c

    lax.fori_loop(1, n, wait_tok, 0)
    everyone = tok_all[...].reshape(total_tokens, CS)
    keys = dot(everyone, proj_v[:, CS : 2 * CS]).astype(BF16)
    scores = dot_t(expanded, keys) * (1.0 / math.sqrt(HDIM))
    scores = scores + extra.reshape(toks * HEADS, total_tokens)
    weights = jnp.exp(scores - jnp.max(scores, axis=-1, keepdims=True))
    denom = jnp.sum(weights, axis=-1, keepdims=True)
    values = dot(everyone, proj_v[:, 2 * CS : 3 * CS]).astype(BF16)
    product = dot(weights.astype(BF16), values) / denom
    mixed = jnp.sum(product.reshape(toks, HEADS, CS) * head_mask[None, :, :], axis=1)
    gated = (mixed * gate).astype(BF16)
    loads["out"].wait()
    tokens_out = (state + dot(gated, v["out"][...])).astype(BF16)
    tokens_out_ref[...] = tokens_out
    loads["back"].wait()
    back = dot(tokens_out, v["back"][...]).astype(BF16)
    back_v[1] = back

    def back_copy(slot, sem, peer):
        return pltpu.make_async_remote_copy(
            src_ref=back_v.at[1],
            dst_ref=back_v.at[slot],
            send_sem=back_send.at[sem],
            recv_sem=back_recv.at[sem],
            device_id={"row": peer},
        )

    ahead = back_copy(0, 0, nxt)
    behind = back_copy(2, 1, prv)

    @pl.when(me < n - 1)
    def _():
        ahead.start()

    @pl.when(me > 0)
    def _():
        behind.start()

    place = (me * rows + iota((1, rows), 1)).astype(F32)
    selects = []
    for offset in (-1, 0, 1):
        begin, end = spans(me + offset, metas[offset][0:1].astype(F32))
        selects.append(((place >= begin) & (place < end)).astype(F32))
    select = jnp.concatenate(selects, axis=0).T.astype(BF16)

    @pl.when(me > 0)
    def _():
        ahead.wait_recv()

    @pl.when(me < n - 1)
    def _():
        behind.wait_recv()

    beside = back_v[...].reshape(3 * toks, CA)
    own_mid = mid[HALO : HALO + rows].astype(F32)
    atoms_out_ref[...] = (own_mid + dot(select, beside)).astype(BF16)

    up.wait_send()
    down.wait_send()

    def drain(k, c):
        meta_copy(k, me).wait_send()
        tok_copy(k, me).wait_send()
        return c

    lax.fori_loop(1, n, drain, 0)

    @pl.when(me < n - 1)
    def _():
        ahead.wait_send()

    @pl.when(me > 0)
    def _():
        behind.wait_send()


def shards(
    n,
    atom_feat,
    window_start,
    atom_count,
    residue_type,
    chain_id,
    token_single,
    pair,
    atom_gain,
    atom_qkv,
    atom_out,
    pool_weight,
    restype_table,
    token_gain,
    token_proj,
    token_out,
    pair_gain,
    pair_bias_weight,
    chain_weight,
    back_weight,
):
    rows, toks = atom_feat.shape[0], token_single.shape[0]
    args = [
        atom_feat,
        window_start.reshape(1, -1),
        atom_count.reshape(1, -1),
        residue_type.reshape(1, -1),
        chain_id.reshape(1, -1),
        token_single,
        pair,
        atom_gain.reshape(1, -1),
        atom_qkv,
        atom_out,
        pool_weight,
        restype_table,
        token_gain.reshape(-1, LANES),
        token_proj,
        token_out,
        pair_gain.reshape(1, -1),
        pair_bias_weight.T,
        chain_weight.reshape(1, -1),
        back_weight,
    ]
    vmem = pl.BlockSpec(memory_space=pltpu.VMEM)
    dma = pltpu.SemaphoreType.DMA
    held = [pltpu.VMEM(x.shape, x.dtype) for x in args]
    held[0] = pltpu.VMEM((rows + 4 * HALO, CA), BF16)
    shapes = (
        jax.ShapeDtypeStruct((rows, CA), BF16),
        jax.ShapeDtypeStruct((toks, CS), BF16),
    )
    results = pl.pallas_call(
        functools.partial(kernel, n),
        out_shape=shapes,
        in_specs=[pl.BlockSpec(memory_space=pltpu.HBM)] * len(args),
        out_specs=(vmem, vmem),
        scratch_shapes=held
        + [
            pltpu.VMEM((8, LANES), jnp.int32),
            pltpu.VMEM((n, 8, LANES), jnp.int32),
            pltpu.VMEM((toks, HEADS, n * toks), F32),
            pltpu.VMEM((n, toks, CS), BF16),
            pltpu.VMEM((3, toks, CA), BF16),
            dma((len(args),)),
            dma((n,)),
            dma((n,)),
            dma((2,)),
            dma((2,)),
            dma((n,)),
            dma((n,)),
            dma((2,)),
            dma((2,)),
        ],
        compiler_params=pltpu.CompilerParams(
            collective_id=0, has_side_effects=True
        ),
    )(*args)
    return pl.pallas_call(
        hand_over,
        out_shape=shapes,
        in_specs=[vmem, vmem],
        out_specs=(vmem, vmem),
        compiler_params=pltpu.CompilerParams(vmem_limit_bytes=4 << 20),
    )(*results)


def hand_over(atoms_ref, tokens_ref, atoms_out_ref, tokens_out_ref):
    atoms_out_ref[...] = atoms_ref[...]
    tokens_out_ref[...] = tokens_ref[...]


def solution(mesh):
    split = P(("groups", "row"))
    return jax.shard_map(
        functools.partial(shards, mesh.shape["row"]),
        mesh=mesh,
        in_specs=(split,) * 7 + (P(),) * 12,
        out_specs=(split, split),
        check_vma=False,
    )
```

```python
import functools
import math

import jax
import jax.numpy as jnp
from jax import lax
from jax.experimental import pallas as pl
from jax.experimental.pallas import tpu as pltpu
from jax.sharding import PartitionSpec as P

CA = 128
CS = 768
HEADS = 16
AHEADS = 4
QBLK = 32
KWIN = 128
HDIM = 48
ADIM = 32
HALO = 64
LANES = 128
F32 = jnp.float32
BF16 = jnp.bfloat16


def iota(shape, dim):
    return lax.broadcasted_iota(jnp.int32, shape, dim)


def layer_norm(values, gain):
    centered = values - jnp.mean(values, axis=-1, keepdims=True)
    variance = jnp.mean(centered * centered, axis=-1, keepdims=True)
    return centered * lax.rsqrt(variance + 1e-05) * gain


def dot(a, b):
    return jnp.dot(a, b, preferred_element_type=F32)


def dot_t(a, b):
    return lax.dot_general(a, b, (((1,), (1,)), ((), ())), preferred_element_type=F32)


NAMES = (
        "feat",
        "window",
        "count",
        "residue",
        "chain",
        "single",
        "pair",
        "atom_gain",
        "atom_qkv",
        "atom_out",
        "pool",
        "table",
        "token_gain",
        "proj",
        "out",
        "pair_gain",
        "pair_weight",
        "chain_weight",
        "back",
    )


def kernel(n, *refs):
    count = len(NAMES)
    hbm = dict(zip(NAMES, refs[:count]))
    atoms_out_ref, tokens_out_ref = refs[count : count + 2]
    v = dict(zip(NAMES, refs[count + 2 : 2 * count + 2]))
    (
        stage,
        meta_all,
        bias_v,
        tok_all,
        back_v,
        local_sem,
        meta_send,
        meta_recv,
        halo_send,
        halo_recv,
        tok_send,
        tok_recv,
        back_send,
        back_recv,
    ) = refs[2 * count + 2 :]
    xbuf = v["feat"]
    feat_hbm = hbm["feat"]
    me = lax.axis_index("row")
    nxt = lax.rem(me + 1, n)
    prv = lax.rem(me + n - 1, n)
    rows = feat_hbm.shape[0]
    toks = hbm["single"].shape[0]
    blocks = rows // QBLK
    edge = 2 * HALO
    total_tokens = n * toks
    total_atoms = n * rows

    barrier = pltpu.get_barrier_semaphore()

    def greet(k, c):
        pl.semaphore_signal(barrier, inc=1, device_id={"row": lax.rem(me + k, n)})
        return c

    lax.fori_loop(1, n, greet, 0)

    loads = {}
    order = (
        "pair",
        "pair_gain",
        "pair_weight",
        "count",
        "chain",
        "window",
        "residue",
        "feat",
        "atom_gain",
        "atom_qkv",
        "atom_out",
        "pool",
        "single",
        "table",
        "token_gain",
        "chain_weight",
        "proj",
        "out",
        "back",
    )
    for i, name in enumerate(order):
        dst = xbuf.at[pl.ds(edge, rows)] if name == "feat" else v[name]
        loads[name] = pltpu.make_async_copy(hbm[name], dst, local_sem.at[i])
        loads[name].start()
    back_v[...] = jnp.zeros_like(back_v)
    stage[...] = jnp.zeros_like(stage)
    for i, name in enumerate(("count", "chain", "window", "residue")):
        loads[name].wait()
        value = v[name][...]
        stage[i : i + 1, : value.shape[1]] = value
    meta_all[me] = stage[...]

    loads["pair"].wait()
    loads["pair_gain"].wait()
    loads["pair_weight"].wait()
    pair_gain = v["pair_gain"][...]
    pair_weight = v["pair_weight"][...]

    def pair_step(t, c):
        normed = layer_norm(v["pair"][t].astype(F32), pair_gain).astype(BF16)
        bias_v[t] = dot_t(pair_weight, normed)
        return c

    for name in ("feat", "atom_gain", "atom_qkv"):
        loads[name].wait()
    head_lane = iota((1, CA), 1) // ADIM

    def project(values):
        normed = layer_norm(values.astype(F32), v["atom_gain"][...]).astype(BF16)
        return dot(normed, v["atom_qkv"][...]).astype(BF16)

    def attend(first_atom, starts, queries, keyvals):
        position = me * rows + (first_atom - HALO) + iota((edge, 2 * edge), 1)
        inside = (
            (position >= starts)
            & (position < starts + KWIN)
            & (position >= 0)
            & (position < total_atoms)
        )
        mixed = jnp.zeros((edge, CA), F32)
        for h in range(AHEADS):
            masked = jnp.where(head_lane == h, queries, jnp.zeros_like(queries))
            scores = dot_t(masked, keyvals[:, :CA]) * (1.0 / math.sqrt(ADIM))
            scores = jnp.where(inside, scores, -1000000000.0)
            weights = jnp.exp(scores - jnp.max(scores, axis=-1, keepdims=True))
            denom = jnp.sum(weights, axis=-1, keepdims=True)
            full = dot(weights.astype(BF16), keyvals[:, CA:]) / denom
            mixed = jnp.where(head_lane == h, full, mixed)
        return mixed.astype(BF16)

    def starts_of(pieces):
        return jnp.concatenate([jnp.broadcast_to(x, (QBLK, 1)) for x in pieces], axis=0)

    own_proj = project(xbuf[edge : edge + rows])
    own_window = v["window"][...]
    per = edge // QBLK
    side = HALO // QBLK
    groups = {}
    for g in range(1, rows // edge):
        at = g * edge - HALO
        first_block = at // QBLK
        starts = starts_of(
            [own_window[:, i : i + 1] for i in range(first_block, first_block + per)]
        )
        groups[g] = attend(
            at, starts, own_proj[at : at + edge, :CA], own_proj[at - HALO : at + edge + HALO, CA:]
        )

    first, second = 0, toks // 4
    pl.semaphore_wait(barrier, n - 1)

    up = pltpu.make_async_remote_copy(
        src_ref=feat_hbm.at[pl.ds(rows - edge, edge)],
        dst_ref=xbuf.at[pl.ds(0, edge)],
        send_sem=halo_send.at[0],
        recv_sem=halo_recv.at[0],
        device_id={"row": nxt},
    )
    down = pltpu.make_async_remote_copy(
        src_ref=feat_hbm.at[pl.ds(0, edge)],
        dst_ref=xbuf.at[pl.ds(edge + rows, edge)],
        send_sem=halo_send.at[1],
        recv_sem=halo_recv.at[1],
        device_id={"row": prv},
    )
    up.start()
    down.start()

    def meta_copy(k, slot):
        return pltpu.make_async_remote_copy(
            src_ref=stage,
            dst_ref=meta_all.at[slot],
            send_sem=meta_send.at[k],
            recv_sem=meta_recv.at[slot],
            device_id={"row": lax.rem(me + k, n)},
        )

    lines = n // 4
    line, seat = lax.div(me, 4), lax.rem(me, 4)
    across = me + 2 - 4 * lax.rem(lax.div(me, 2), 2)
    sibling = me + 1 - 2 * lax.rem(me, 2)
    across_seat = lax.rem(across, 4)
    sibling_seat = lax.rem(sibling, 4)
    corner_seat = 3 - seat

    def slot_of(k, place):
        return 4 * lax.rem(line + k, lines) + place

    def tok_copy(sem, slot, peer):
        return pltpu.make_async_remote_copy(
            src_ref=tok_all.at[slot],
            dst_ref=tok_all.at[slot],
            send_sem=tok_send.at[sem],
            recv_sem=tok_recv.at[slot],
            device_id={"row": peer},
        )

    def along_line(k):
        return tok_copy(k, me, slot_of(k, seat))

    def to_across(k):
        return tok_copy(lines + k, slot_of(k, seat), across)

    def to_sibling(k):
        return tok_copy(2 * lines + k, slot_of(k, seat), sibling)

    def corner(k):
        return tok_copy(3 * lines + k, slot_of(k, across_seat), sibling)

    def diagonal(k):
        return tok_copy(lines + k, me, slot_of(k, across_seat))

    def arrived(k, place):
        tok_copy(0, slot_of(k, place), sibling).wait_recv()

    def start_meta(k, c):
        meta_copy(k, me).start()
        return c

    lax.fori_loop(1, n, start_meta, 0)

    lax.fori_loop(first, second, pair_step, 0, unroll=4)

    for name in ("atom_out", "pool"):
        loads[name].wait()
    up.wait_recv()
    down.wait_recv()

    def wait_meta(k, c):
        meta_copy(k, lax.rem(me + k, n)).wait_recv()
        return c

    wait_meta(1, 0)
    wait_meta(n - 1, 0)
    metas = {-1: meta_all[prv], 0: meta_all[me], 1: meta_all[nxt]}
    low = project(xbuf[:edge])
    starts = starts_of(
        [metas[-1][2:3, i : i + 1] for i in range(blocks - side, blocks)]
        + [own_window[:, i : i + 1] for i in range(per - side)]
    )
    keyvals = jnp.concatenate([low[:, CA:], own_proj[:edge, CA:]], axis=0)
    queries = jnp.concatenate([low[edge - HALO :, :CA], own_proj[: edge - HALO, :CA]], axis=0)
    groups[0] = attend(-HALO, starts, queries, keyvals)
    high = project(xbuf[edge + rows :])
    starts = starts_of(
        [own_window[:, i : i + 1] for i in range(blocks - per + side, blocks)]
        + [metas[1][2:3, i : i + 1] for i in range(side)]
    )
    keyvals = jnp.concatenate([own_proj[rows - edge :, CA:], high[:, CA:]], axis=0)
    queries = jnp.concatenate([own_proj[rows - edge + HALO :, :CA], high[:HALO, :CA]], axis=0)
    groups[rows // edge] = attend(rows - edge + HALO, starts, queries, keyvals)
    ext = xbuf[HALO : 3 * HALO + rows].astype(F32)
    lax.fori_loop(2, n - 1, wait_meta, 0)
    attended = jnp.concatenate([groups[g] for g in range(rows // edge + 1)], axis=0)
    mid = (ext + dot(attended, v["atom_out"][...])).astype(BF16)

    lifted = jax.nn.relu(dot(mid, v["pool"][...])).astype(BF16)

    counts_f = meta_all[:, 0, :].astype(F32)
    source = iota((n, LANES), 0)
    count_lane = iota((n, LANES), 1) < toks
    tok_row = iota((toks, LANES), 0)
    tok_lane = iota((toks, LANES), 1)

    def column(row):
        return jnp.sum(jnp.where(tok_lane == tok_row, row, 0.0), axis=1, keepdims=True)

    def spans(device, row):
        prior = jnp.where((source < device) & count_lane, counts_f, 0.0)
        prior = jnp.sum(jnp.sum(prior, axis=1, keepdims=True), axis=0, keepdims=True)
        begin = prior + jnp.sum(jnp.where(tok_lane < tok_row, row, 0.0), axis=1, keepdims=True)
        return begin, begin + column(row)

    own_meta = metas[0].astype(F32)
    own_row = own_meta[0:1]
    begin, end = spans(me, own_row)
    place = (me * rows - HALO + iota((1, rows + 2 * HALO), 1)).astype(F32)
    select = ((place >= begin) & (place < end)).astype(F32).astype(BF16)
    pooled = dot(select, lifted)
    kinds = hbm["table"].shape[0]
    onehot = (
        (iota((toks, kinds), 1).astype(F32) == column(own_meta[3:4])).astype(F32).astype(BF16)
    )
    for name in ("single", "table", "token_gain", "chain_weight"):
        loads[name].wait()
    state = v["single"][...].astype(F32) + pooled / column(own_row)
    state = state + dot(onehot, v["table"][...])
    gain = v["token_gain"][...]
    gain = jnp.concatenate([gain[i : i + 1] for i in range(gain.shape[0])], axis=1)
    token_normed = layer_norm(state, gain).astype(BF16)
    tok_all[me] = token_normed

    def start_tok(k, c):
        along_line(k).start()
        diagonal(k).start()
        return c

    lax.fori_loop(1, lines, start_tok, 0)
    to_across(0).start()
    to_sibling(0).start()

    loads["proj"].wait()
    proj_v = v["proj"]
    query = dot(token_normed, proj_v[:, :CS]).astype(BF16).astype(F32)
    gate = jax.nn.sigmoid(dot(token_normed, proj_v[:, 3 * CS :]))
    column_of = iota((HEADS, CS), 1)
    head_row = iota((HEADS, CS), 0) * HDIM
    head_mask = ((column_of >= head_row) & (column_of < head_row + HDIM)).astype(F32)
    expanded = (query[:, None, :] * head_mask[None, :, :]).reshape(toks * HEADS, CS).astype(BF16)

    shift = toks.bit_length() - 1
    token_of = iota((LANES, total_tokens), 1)
    pick = (iota((LANES, total_tokens), 0) == (token_of & (toks - 1))).astype(F32)
    chains = dot(meta_all[:, 1, :].astype(F32).astype(BF16), pick.astype(BF16))
    owner = iota((n, total_tokens), 1) >> shift
    chains = jnp.sum(
        jnp.where(owner == iota((n, total_tokens), 0), chains, 0.0), axis=0, keepdims=True
    )
    same = (chains == column(own_meta[1:2])).astype(F32)
    eye = iota((HEADS, HEADS), 0) == iota((HEADS, HEADS), 1)
    chain_weight = jnp.sum(
        jnp.where(eye, v["chain_weight"][...], 0.0), axis=1, keepdims=True
    )
    lax.fori_loop(second, toks, pair_step, 0, unroll=4)
    extra = bias_v[...] + same[:, None, :] * chain_weight[None, :, :]

    def pass_line(k, c):
        arrived(k, seat)
        to_sibling(k).start()
        return c

    lax.fori_loop(1, lines, pass_line, 0)

    def pass_across(k, c):
        arrived(k, across_seat)
        corner(k).start()
        return c

    lax.fori_loop(0, lines, pass_across, 0)

    def take(k, c):
        arrived(k, sibling_seat)
        arrived(k, corner_seat)
        return c

    lax.fori_loop(0, lines, take, 0)
    everyone = tok_all[...].reshape(total_tokens, CS)
    keys = dot(everyone, proj_v[:, CS : 2 * CS]).astype(BF16)
    scores = dot_t(expanded, keys) * (1.0 / math.sqrt(HDIM))
    scores = scores + extra.reshape(toks * HEADS, total_tokens)
    weights = jnp.exp(scores - jnp.max(scores, axis=-1, keepdims=True))
    denom = jnp.sum(weights, axis=-1, keepdims=True)
    values = dot(everyone, proj_v[:, 2 * CS : 3 * CS]).astype(BF16)
    product = dot(weights.astype(BF16), values) / denom
    mixed = jnp.sum(product.reshape(toks, HEADS, CS) * head_mask[None, :, :], axis=1)
    gated = (mixed * gate).astype(BF16)
    loads["out"].wait()
    tokens_out = (state + dot(gated, v["out"][...])).astype(BF16)
    tokens_out_ref[...] = tokens_out
    loads["back"].wait()
    back = dot(tokens_out, v["back"][...]).astype(BF16)
    back_v[1] = back

    def back_copy(slot, sem, peer):
        return pltpu.make_async_remote_copy(
            src_ref=back_v.at[1],
            dst_ref=back_v.at[slot],
            send_sem=back_send.at[sem],
            recv_sem=back_recv.at[sem],
            device_id={"row": peer},
        )

    ahead = back_copy(0, 0, nxt)
    behind = back_copy(2, 1, prv)

    @pl.when(me < n - 1)
    def _():
        ahead.start()

    @pl.when(me > 0)
    def _():
        behind.start()

    place = (me * rows + iota((1, rows), 1)).astype(F32)
    selects = []
    for offset in (-1, 0, 1):
        begin, end = spans(me + offset, metas[offset][0:1].astype(F32))
        selects.append(((place >= begin) & (place < end)).astype(F32))
    select = jnp.concatenate(selects, axis=0).T.astype(BF16)

    @pl.when(me > 0)
    def _():
        ahead.wait_recv()

    @pl.when(me < n - 1)
    def _():
        behind.wait_recv()

    beside = back_v[...].reshape(3 * toks, CA)
    own_mid = mid[HALO : HALO + rows].astype(F32)
    atoms_out_ref[...] = (own_mid + dot(select, beside)).astype(BF16)

    up.wait_send()
    down.wait_send()

    def drain(k, c):
        meta_copy(k, me).wait_send()
        return c

    lax.fori_loop(1, n, drain, 0)

    def drain_line(k, c):
        along_line(k).wait_send()
        return c

    lax.fori_loop(1, lines, drain_line, 0)

    def drain_rest(k, c):
        diagonal(k).wait_send()
        to_sibling(k).wait_send()
        corner(k).wait_send()
        return c

    lax.fori_loop(0, lines, drain_rest, 0)

    @pl.when(me < n - 1)
    def _():
        ahead.wait_send()

    @pl.when(me > 0)
    def _():
        behind.wait_send()


def shards(
    n,
    atom_feat,
    window_start,
    atom_count,
    residue_type,
    chain_id,
    token_single,
    pair,
    atom_gain,
    atom_qkv,
    atom_out,
    pool_weight,
    restype_table,
    token_gain,
    token_proj,
    token_out,
    pair_gain,
    pair_bias_weight,
    chain_weight,
    back_weight,
):
    rows, toks = atom_feat.shape[0], token_single.shape[0]
    args = [
        atom_feat,
        window_start.reshape(1, -1),
        atom_count.reshape(1, -1),
        residue_type.reshape(1, -1),
        chain_id.reshape(1, -1),
        token_single,
        pair,
        atom_gain.reshape(1, -1),
        atom_qkv,
        atom_out,
        pool_weight,
        restype_table,
        token_gain.reshape(-1, LANES),
        token_proj,
        token_out,
        pair_gain.reshape(1, -1),
        pair_bias_weight.T,
        chain_weight.reshape(1, -1),
        back_weight,
    ]
    vmem = pl.BlockSpec(memory_space=pltpu.VMEM)
    dma = pltpu.SemaphoreType.DMA
    held = [pltpu.VMEM(x.shape, x.dtype) for x in args]
    held[0] = pltpu.VMEM((rows + 4 * HALO, CA), BF16)
    shapes = (
        jax.ShapeDtypeStruct((rows, CA), BF16),
        jax.ShapeDtypeStruct((toks, CS), BF16),
    )
    results = pl.pallas_call(
        functools.partial(kernel, n),
        out_shape=shapes,
        in_specs=[pl.BlockSpec(memory_space=pltpu.HBM)] * len(args),
        out_specs=(vmem, vmem),
        scratch_shapes=held
        + [
            pltpu.VMEM((8, LANES), jnp.int32),
            pltpu.VMEM((n, 8, LANES), jnp.int32),
            pltpu.VMEM((toks, HEADS, n * toks), F32),
            pltpu.VMEM((n, toks, CS), BF16),
            pltpu.VMEM((3, toks, CA), BF16),
            dma((len(args),)),
            dma((n,)),
            dma((n,)),
            dma((2,)),
            dma((2,)),
            dma((n,)),
            dma((n,)),
            dma((2,)),
            dma((2,)),
        ],
        compiler_params=pltpu.CompilerParams(
            collective_id=0, has_side_effects=True, vmem_limit_bytes=48 << 20
        ),
    )(*[pltpu.with_memory_space_constraint(x, pltpu.HBM) for x in args])
    return pl.pallas_call(
        hand_over,
        out_shape=shapes,
        in_specs=[vmem, vmem],
        out_specs=(vmem, vmem),
        compiler_params=pltpu.CompilerParams(vmem_limit_bytes=4 << 20),
    )(*results)


def hand_over(atoms_ref, tokens_ref, atoms_out_ref, tokens_out_ref):
    atoms_out_ref[...] = atoms_ref[...]
    tokens_out_ref[...] = tokens_ref[...]


def solution(mesh):
    split = P(("groups", "row"))
    return jax.shard_map(
        functools.partial(shards, mesh.shape["row"]),
        mesh=mesh,
        in_specs=(split,) * 7 + (P(),) * 12,
        out_specs=(split, split),
        check_vma=False,
    )
```

```python
import functools
import math

import jax
import jax.numpy as jnp
from jax import lax
from jax.experimental import pallas as pl
from jax.experimental.pallas import tpu as pltpu
from jax.sharding import PartitionSpec as P

CA = 128
CS = 768
HEADS = 16
AHEADS = 4
QBLK = 32
KWIN = 128
HDIM = 48
ADIM = 32
HALO = 64
LANES = 128
F32 = jnp.float32
BF16 = jnp.bfloat16


def iota(shape, dim):
    return lax.broadcasted_iota(jnp.int32, shape, dim)


def layer_norm(values, gain):
    centered = values - jnp.mean(values, axis=-1, keepdims=True)
    variance = jnp.mean(centered * centered, axis=-1, keepdims=True)
    return centered * lax.rsqrt(variance + 1e-05) * gain


def dot(a, b):
    return jnp.dot(a, b, preferred_element_type=F32)


def dot_t(a, b):
    return lax.dot_general(a, b, (((1,), (1,)), ((), ())), preferred_element_type=F32)


NAMES = (
        "feat",
        "window",
        "count",
        "residue",
        "chain",
        "single",
        "pair",
        "atom_gain",
        "atom_qkv",
        "atom_out",
        "pool",
        "table",
        "token_gain",
        "proj",
        "out",
        "pair_gain",
        "pair_weight",
        "chain_weight",
        "back",
    )


def kernel(n, *refs):
    count = len(NAMES)
    hbm = dict(zip(NAMES, refs[:count]))
    atoms_out_ref, tokens_out_ref = refs[count : count + 2]
    v = dict(zip(NAMES, refs[count + 2 : 2 * count + 2]))
    (
        stage,
        meta_all,
        bias_v,
        tok_all,
        back_v,
        local_sem,
        meta_send,
        meta_recv,
        halo_send,
        halo_recv,
        tok_send,
        tok_recv,
        back_send,
        back_recv,
    ) = refs[2 * count + 2 :]
    xbuf = v["feat"]
    feat_hbm = hbm["feat"]
    me = lax.axis_index("row")
    nxt = lax.rem(me + 1, n)
    prv = lax.rem(me + n - 1, n)
    rows = feat_hbm.shape[0]
    toks = hbm["single"].shape[0]
    blocks = rows // QBLK
    edge = 2 * HALO
    total_tokens = n * toks
    total_atoms = n * rows

    barrier = pltpu.get_barrier_semaphore()

    def greet(k, c):
        pl.semaphore_signal(barrier, inc=1, device_id={"row": lax.rem(me + k, n)})
        return c

    lax.fori_loop(1, n, greet, 0)

    loads = {}
    order = (
        "pair",
        "pair_gain",
        "pair_weight",
        "count",
        "chain",
        "window",
        "residue",
        "feat",
        "atom_gain",
        "atom_qkv",
        "atom_out",
        "pool",
        "single",
        "table",
        "token_gain",
        "chain_weight",
        "proj",
        "out",
        "back",
    )
    for i, name in enumerate(order):
        dst = xbuf.at[pl.ds(edge, rows)] if name == "feat" else v[name]
        loads[name] = pltpu.make_async_copy(hbm[name], dst, local_sem.at[i])
        loads[name].start()
    back_v[...] = jnp.zeros_like(back_v)
    stage[...] = jnp.zeros_like(stage)
    for i, name in enumerate(("count", "chain", "window", "residue")):
        loads[name].wait()
        value = v[name][...]
        stage[i : i + 1, : value.shape[1]] = value
    meta_all[me] = stage[...]

    loads["pair"].wait()
    loads["pair_gain"].wait()
    loads["pair_weight"].wait()
    pair_gain = v["pair_gain"][...]
    pair_weight = v["pair_weight"][...]

    def pair_step(t, c):
        normed = layer_norm(v["pair"][t].astype(F32), pair_gain).astype(BF16)
        bias_v[t] = dot_t(pair_weight, normed)
        return c

    for name in ("feat", "atom_gain", "atom_qkv"):
        loads[name].wait()
    head_lane = iota((1, CA), 1) // ADIM

    def project(values):
        normed = layer_norm(values.astype(F32), v["atom_gain"][...]).astype(BF16)
        return dot(normed, v["atom_qkv"][...]).astype(BF16)

    def attend(first_atom, starts, queries, keyvals):
        position = me * rows + (first_atom - HALO) + iota((edge, 2 * edge), 1)
        inside = (
            (position >= starts)
            & (position < starts + KWIN)
            & (position >= 0)
            & (position < total_atoms)
        )
        mixed = jnp.zeros((edge, CA), F32)
        for h in range(AHEADS):
            masked = jnp.where(head_lane == h, queries, jnp.zeros_like(queries))
            scores = dot_t(masked, keyvals[:, :CA]) * (1.0 / math.sqrt(ADIM))
            scores = jnp.where(inside, scores, -1000000000.0)
            weights = jnp.exp(scores - jnp.max(scores, axis=-1, keepdims=True))
            denom = jnp.sum(weights, axis=-1, keepdims=True)
            full = dot(weights.astype(BF16), keyvals[:, CA:]) / denom
            mixed = jnp.where(head_lane == h, full, mixed)
        return mixed.astype(BF16)

    def starts_of(pieces):
        return jnp.concatenate([jnp.broadcast_to(x, (QBLK, 1)) for x in pieces], axis=0)

    own_proj = project(xbuf[edge : edge + rows])
    own_window = v["window"][...]
    per = edge // QBLK
    side = HALO // QBLK
    groups = {}
    for g in range(1, rows // edge):
        at = g * edge - HALO
        first_block = at // QBLK
        starts = starts_of(
            [own_window[:, i : i + 1] for i in range(first_block, first_block + per)]
        )
        groups[g] = attend(
            at, starts, own_proj[at : at + edge, :CA], own_proj[at - HALO : at + edge + HALO, CA:]
        )

    first, second = 0, 3 * toks // 4
    pl.semaphore_wait(barrier, n - 1)

    up = pltpu.make_async_remote_copy(
        src_ref=feat_hbm.at[pl.ds(rows - edge, edge)],
        dst_ref=xbuf.at[pl.ds(0, edge)],
        send_sem=halo_send.at[0],
        recv_sem=halo_recv.at[0],
        device_id={"row": nxt},
    )
    down = pltpu.make_async_remote_copy(
        src_ref=feat_hbm.at[pl.ds(0, edge)],
        dst_ref=xbuf.at[pl.ds(edge + rows, edge)],
        send_sem=halo_send.at[1],
        recv_sem=halo_recv.at[1],
        device_id={"row": prv},
    )
    up.start()
    down.start()

    def meta_copy(k, slot):
        return pltpu.make_async_remote_copy(
            src_ref=stage,
            dst_ref=meta_all.at[slot],
            send_sem=meta_send.at[k],
            recv_sem=meta_recv.at[slot],
            device_id={"row": lax.rem(me + k, n)},
        )

    lines = n // 4
    line, seat = lax.div(me, 4), lax.rem(me, 4)
    across = me + 2 - 4 * lax.rem(lax.div(me, 2), 2)
    sibling = me + 1 - 2 * lax.rem(me, 2)
    across_seat = lax.rem(across, 4)
    sibling_seat = lax.rem(sibling, 4)
    corner_seat = 3 - seat

    def slot_of(k, place):
        return 4 * lax.rem(line + k, lines) + place

    def tok_copy(sem, slot, peer):
        return pltpu.make_async_remote_copy(
            src_ref=tok_all.at[slot],
            dst_ref=tok_all.at[slot],
            send_sem=tok_send.at[sem],
            recv_sem=tok_recv.at[slot],
            device_id={"row": peer},
        )

    def along_line(k):
        return tok_copy(k, me, slot_of(k, seat))

    def to_across(k):
        return tok_copy(lines + k, slot_of(k, seat), across)

    def to_sibling(k):
        return tok_copy(2 * lines + k, slot_of(k, seat), sibling)

    def corner(k):
        return tok_copy(3 * lines + k, slot_of(k, across_seat), sibling)

    def diagonal(k):
        return tok_copy(lines + k, me, slot_of(k, across_seat))

    def arrived(k, place):
        tok_copy(0, slot_of(k, place), sibling).wait_recv()

    def start_meta(k, c):
        meta_copy(k, me).start()
        return c

    lax.fori_loop(1, n, start_meta, 0)

    lax.fori_loop(first, second, pair_step, 0, unroll=4)

    for name in ("atom_out", "pool"):
        loads[name].wait()
    up.wait_recv()
    down.wait_recv()

    def wait_meta(k, c):
        meta_copy(k, lax.rem(me + k, n)).wait_recv()
        return c

    wait_meta(1, 0)
    wait_meta(n - 1, 0)
    metas = {-1: meta_all[prv], 0: meta_all[me], 1: meta_all[nxt]}
    low = project(xbuf[:edge])
    starts = starts_of(
        [metas[-1][2:3, i : i + 1] for i in range(blocks - side, blocks)]
        + [own_window[:, i : i + 1] for i in range(per - side)]
    )
    keyvals = jnp.concatenate([low[:, CA:], own_proj[:edge, CA:]], axis=0)
    queries = jnp.concatenate([low[edge - HALO :, :CA], own_proj[: edge - HALO, :CA]], axis=0)
    groups[0] = attend(-HALO, starts, queries, keyvals)
    high = project(xbuf[edge + rows :])
    starts = starts_of(
        [own_window[:, i : i + 1] for i in range(blocks - per + side, blocks)]
        + [metas[1][2:3, i : i + 1] for i in range(side)]
    )
    keyvals = jnp.concatenate([own_proj[rows - edge :, CA:], high[:, CA:]], axis=0)
    queries = jnp.concatenate([own_proj[rows - edge + HALO :, :CA], high[:HALO, :CA]], axis=0)
    groups[rows // edge] = attend(rows - edge + HALO, starts, queries, keyvals)
    ext = xbuf[HALO : 3 * HALO + rows].astype(F32)
    lax.fori_loop(2, n - 1, wait_meta, 0)
    attended = jnp.concatenate([groups[g] for g in range(rows // edge + 1)], axis=0)
    mid = (ext + dot(attended, v["atom_out"][...])).astype(BF16)

    lifted = jax.nn.relu(dot(mid, v["pool"][...])).astype(BF16)

    counts_f = meta_all[:, 0, :].astype(F32)
    source = iota((n, LANES), 0)
    count_lane = iota((n, LANES), 1) < toks
    tok_row = iota((toks, LANES), 0)
    tok_lane = iota((toks, LANES), 1)

    def column(row):
        return jnp.sum(jnp.where(tok_lane == tok_row, row, 0.0), axis=1, keepdims=True)

    def spans(device, row):
        prior = jnp.where((source < device) & count_lane, counts_f, 0.0)
        prior = jnp.sum(jnp.sum(prior, axis=1, keepdims=True), axis=0, keepdims=True)
        begin = prior + jnp.sum(jnp.where(tok_lane < tok_row, row, 0.0), axis=1, keepdims=True)
        return begin, begin + column(row)

    own_meta = metas[0].astype(F32)
    own_row = own_meta[0:1]
    begin, end = spans(me, own_row)
    place = (me * rows - HALO + iota((1, rows + 2 * HALO), 1)).astype(F32)
    select = ((place >= begin) & (place < end)).astype(F32).astype(BF16)
    pooled = dot(select, lifted)
    kinds = hbm["table"].shape[0]
    onehot = (
        (iota((toks, kinds), 1).astype(F32) == column(own_meta[3:4])).astype(F32).astype(BF16)
    )
    for name in ("single", "table", "token_gain", "chain_weight"):
        loads[name].wait()
    state = v["single"][...].astype(F32) + pooled / column(own_row)
    state = state + dot(onehot, v["table"][...])
    gain = v["token_gain"][...]
    gain = jnp.concatenate([gain[i : i + 1] for i in range(gain.shape[0])], axis=1)
    token_normed = layer_norm(state, gain).astype(BF16)
    tok_all[me] = token_normed

    def start_tok(k, c):
        along_line(k).start()
        diagonal(k).start()
        return c

    to_sibling(0).start()
    to_across(0).start()
    lax.fori_loop(1, lines, start_tok, 0)

    loads["proj"].wait()
    proj_v = v["proj"]
    query = dot(token_normed, proj_v[:, :CS]).astype(BF16).astype(F32)
    gate = jax.nn.sigmoid(dot(token_normed, proj_v[:, 3 * CS :]))
    column_of = iota((HEADS, CS), 1)
    head_row = iota((HEADS, CS), 0) * HDIM
    head_mask = ((column_of >= head_row) & (column_of < head_row + HDIM)).astype(F32)
    expanded = (query[:, None, :] * head_mask[None, :, :]).reshape(toks * HEADS, CS).astype(BF16)

    absorbed = dot_t(expanded, proj_v[:, CS : 2 * CS]).astype(BF16)

    shift = toks.bit_length() - 1
    token_of = iota((LANES, total_tokens), 1)
    pick = (iota((LANES, total_tokens), 0) == (token_of & (toks - 1))).astype(F32)
    chains = dot(meta_all[:, 1, :].astype(F32).astype(BF16), pick.astype(BF16))
    owner = iota((n, total_tokens), 1) >> shift
    chains = jnp.sum(
        jnp.where(owner == iota((n, total_tokens), 0), chains, 0.0), axis=0, keepdims=True
    )
    same = (chains == column(own_meta[1:2])).astype(F32)
    eye = iota((HEADS, HEADS), 0) == iota((HEADS, HEADS), 1)
    chain_weight = jnp.sum(
        jnp.where(eye, v["chain_weight"][...], 0.0), axis=1, keepdims=True
    )
    lax.fori_loop(second, toks, pair_step, 0, unroll=4)
    extra = bias_v[...] + same[:, None, :] * chain_weight[None, :, :]

    def pass_line(k, c):
        arrived(k, seat)
        to_sibling(k).start()
        return c

    lax.fori_loop(1, lines, pass_line, 0)

    def pass_across(k, c):
        arrived(k, across_seat)
        corner(k).start()
        return c

    lax.fori_loop(0, lines, pass_across, 0)

    def take(k, c):
        arrived(k, sibling_seat)
        arrived(k, corner_seat)
        return c

    lax.fori_loop(0, lines, take, 0)
    everyone = tok_all[...].reshape(total_tokens, CS)
    scores = dot_t(absorbed, everyone) * (1.0 / math.sqrt(HDIM))
    scores = scores + extra.reshape(toks * HEADS, total_tokens)
    weights = jnp.exp(scores - jnp.max(scores, axis=-1, keepdims=True))
    denom = jnp.sum(weights, axis=-1, keepdims=True)
    values = dot(everyone, proj_v[:, 2 * CS : 3 * CS]).astype(BF16)
    product = dot(weights.astype(BF16), values) / denom
    mixed = jnp.sum(product.reshape(toks, HEADS, CS) * head_mask[None, :, :], axis=1)
    gated = (mixed * gate).astype(BF16)
    loads["out"].wait()
    tokens_out = (state + dot(gated, v["out"][...])).astype(BF16)
    tokens_out_ref[...] = tokens_out
    loads["back"].wait()
    back = dot(tokens_out, v["back"][...]).astype(BF16)
    back_v[1] = back

    def back_copy(slot, sem, peer):
        return pltpu.make_async_remote_copy(
            src_ref=back_v.at[1],
            dst_ref=back_v.at[slot],
            send_sem=back_send.at[sem],
            recv_sem=back_recv.at[sem],
            device_id={"row": peer},
        )

    ahead = back_copy(0, 0, nxt)
    behind = back_copy(2, 1, prv)

    @pl.when(me < n - 1)
    def _():
        ahead.start()

    @pl.when(me > 0)
    def _():
        behind.start()

    place = (me * rows + iota((1, rows), 1)).astype(F32)
    selects = []
    for offset in (-1, 0, 1):
        begin, end = spans(me + offset, metas[offset][0:1].astype(F32))
        selects.append(((place >= begin) & (place < end)).astype(F32))
    select = jnp.concatenate(selects, axis=0).T.astype(BF16)

    @pl.when(me > 0)
    def _():
        ahead.wait_recv()

    @pl.when(me < n - 1)
    def _():
        behind.wait_recv()

    beside = back_v[...].reshape(3 * toks, CA)
    own_mid = mid[HALO : HALO + rows].astype(F32)
    atoms_out_ref[...] = (own_mid + dot(select, beside)).astype(BF16)

    up.wait_send()
    down.wait_send()

    def drain(k, c):
        meta_copy(k, me).wait_send()
        return c

    lax.fori_loop(1, n, drain, 0)

    def drain_line(k, c):
        along_line(k).wait_send()
        return c

    lax.fori_loop(1, lines, drain_line, 0)

    def drain_rest(k, c):
        diagonal(k).wait_send()
        to_sibling(k).wait_send()
        corner(k).wait_send()
        return c

    lax.fori_loop(0, lines, drain_rest, 0)

    @pl.when(me < n - 1)
    def _():
        ahead.wait_send()

    @pl.when(me > 0)
    def _():
        behind.wait_send()


def shards(
    n,
    atom_feat,
    window_start,
    atom_count,
    residue_type,
    chain_id,
    token_single,
    pair,
    atom_gain,
    atom_qkv,
    atom_out,
    pool_weight,
    restype_table,
    token_gain,
    token_proj,
    token_out,
    pair_gain,
    pair_bias_weight,
    chain_weight,
    back_weight,
):
    rows, toks = atom_feat.shape[0], token_single.shape[0]
    args = [
        atom_feat,
        window_start.reshape(1, -1),
        atom_count.reshape(1, -1),
        residue_type.reshape(1, -1),
        chain_id.reshape(1, -1),
        token_single,
        pair,
        atom_gain.reshape(1, -1),
        atom_qkv,
        atom_out,
        pool_weight,
        restype_table,
        token_gain.reshape(-1, LANES),
        token_proj,
        token_out,
        pair_gain.reshape(1, -1),
        pair_bias_weight.T,
        chain_weight.reshape(1, -1),
        back_weight,
    ]
    vmem = pl.BlockSpec(memory_space=pltpu.VMEM)
    dma = pltpu.SemaphoreType.DMA
    held = [pltpu.VMEM(x.shape, x.dtype) for x in args]
    held[0] = pltpu.VMEM((rows + 4 * HALO, CA), BF16)
    shapes = (
        jax.ShapeDtypeStruct((rows, CA), BF16),
        jax.ShapeDtypeStruct((toks, CS), BF16),
    )
    results = pl.pallas_call(
        functools.partial(kernel, n),
        out_shape=shapes,
        in_specs=[pl.BlockSpec(memory_space=pltpu.HBM)] * len(args),
        out_specs=(vmem, vmem),
        scratch_shapes=held
        + [
            pltpu.VMEM((8, LANES), jnp.int32),
            pltpu.VMEM((n, 8, LANES), jnp.int32),
            pltpu.VMEM((toks, HEADS, n * toks), F32),
            pltpu.VMEM((n, toks, CS), BF16),
            pltpu.VMEM((3, toks, CA), BF16),
            dma((len(args),)),
            dma((n,)),
            dma((n,)),
            dma((2,)),
            dma((2,)),
            dma((n,)),
            dma((n,)),
            dma((2,)),
            dma((2,)),
        ],
        compiler_params=pltpu.CompilerParams(
            collective_id=0, has_side_effects=True, vmem_limit_bytes=48 << 20
        ),
    )(*[pltpu.with_memory_space_constraint(x, pltpu.HBM) for x in args])
    return pl.pallas_call(
        hand_over,
        out_shape=shapes,
        in_specs=[vmem, vmem],
        out_specs=(vmem, vmem),
        compiler_params=pltpu.CompilerParams(vmem_limit_bytes=4 << 20),
    )(*results)


def hand_over(atoms_ref, tokens_ref, atoms_out_ref, tokens_out_ref):
    atoms_out_ref[...] = atoms_ref[...]
    tokens_out_ref[...] = tokens_ref[...]


def solution(mesh):
    split = P(("groups", "row"))
    return jax.shard_map(
        functools.partial(shards, mesh.shape["row"]),
        mesh=mesh,
        in_specs=(split,) * 7 + (P(),) * 12,
        out_specs=(split, split),
        check_vma=False,
    )
```
